32 devices in a mesh: row: 4 (over x, core), col: 8 (over z, y).
Axes of the slice: x: 2, y: 2, z: 4, core: 2. Of those that a mesh axis runs over, the one named last changes fastest.
Arguments:
- velocity: float32 [3, 16, 2048, 1024], P(None, None, 'col', 'row'), may hold values from -6 to 6
- z_inverse: float32 [1024, 1024], replicated, may hold values from -0.1875 to 0.1875
- tiles: int32 [256, 4], P(('row', 'col')), may hold values from 0 to 4095, as said below
- amplitude: float32 [256, 4, 256], P(('row', 'col')), may hold values from -3 to 3
- lateral: float32 [256, 8, 256], P(('row', 'col')), may hold values from -2 to 2
- vertical: float32 [256, 256, 256], P(('row', 'col')), may hold values from -0.375 to 0.375
- wall_velocity: float32 [256, 3, 256], P(('row', 'col')), may hold values from -6 to 6
- surface: float32 [256, 256], P(('row', 'col')), may hold values from 0.5 to 2
Outputs:
- spectrum: float32 [2, 3, 16, 1024, 1024], P(None, None, 'row', 'col')
- marker_force: float32 [256, 3, 256], P(('row', 'col'))
The draws below stay inside these ranges and needn't reach their ends.
Inputs may be any that keep to these rules, and one draw needn't show every extreme that they name: tiles[b, k] is a tile id in block b's row group; the column index holding tile t is t // 512. Among the 32 entries of one device's blocks, at most 8 (repeats counted) name tiles held by one column index.
All inputs are finite; a program needn't handle non-finite values.
Results may differ from the reference program's by a relative error of at most 0.000071.
Values sent between devices are 32-bit elements; how exact they have to be, the bound alone decides.
No kernel may reach another device: no remote copies, remote signals or barrier semaphores. Data moves between devices by JAX's collectives and lax.ppermute only.
A program may use at most 128 MiB of HBM per device.

```python
import math
import jax
import jax.numpy as jnp
from jax import lax

NY = 2048
NZ = 1024
TY = 8
K = 4
BLOCK = 256
BLK_DEV = 8
XW = 16
TZ = 256
YTD = 32
T_DEV = 512
BLOCKS = 256
N_ROW = 4
N_COL = 8


def draw_tiles(key, part):
    devices = N_ROW * N_COL
    request_count = BLK_DEV * K
    keys = jax.random.split(key, 4)
    hot_column = jax.random.randint(keys[0], (N_ROW,), 0, N_COL)
    hot_device = jnp.repeat(hot_column, N_COL)
    columns = jnp.arange(N_COL, dtype=jnp.int32)[None, :]
    scores = jax.random.randint(keys[1], (devices, N_COL), 0, 1 << 20) * N_COL + columns
    scores = jnp.where(columns == hot_device[:, None], (1 << 20) * N_COL + N_COL, scores)
    chosen = jnp.argsort(-scores, axis=1)[:, :4]

    def shuffled(one_key):
        return jax.random.permutation(one_key, request_count)
    order = jax.vmap(shuffled)(jax.random.split(keys[2], devices))
    holder = jnp.take_along_axis(chosen, order % 4, axis=1)
    within = jax.random.randint(keys[3], (devices, request_count), 0, T_DEV)
    return (holder * T_DEV + within).astype(jnp.int32).reshape(devices * BLK_DEV, K)


def levels(own_key, dims, cuts, smallest, high):
    loudness = 1.0
    for dim, shards_of in cuts:
        steps = jax.random.uniform(jax.random.fold_in(jax.random.fold_in(own_key, 6), dim), (shards_of,), jnp.float32, smallest / len(cuts), high / len(cuts))
        loudness = loudness * jnp.repeat(jnp.exp(steps), dims[dim] // shards_of).reshape((-1,) + (1,) * (len(dims) - 1 - dim))
    return loudness


def scatter_about(rng, dims, width, reach, cuts=(), kind=jnp.bfloat16):
    drawn = jax.random.normal(rng, dims, jnp.float32) * width
    if len(cuts) > 0:
        drawn = levels(rng, dims, cuts, -0.22, 0.18) * drawn
    return jnp.clip(drawn, min=-reach, max=reach).astype(kind)


def setup_inputs(seed: int = 0) -> dict:
    key_of = jax.random.split(jax.random.key(seed), 9)
    return {
        "velocity": scatter_about(key_of[0], (3, XW, NY, NZ), 1.0, 6.0, ((2, 8), (3, 4)), jnp.float32),
        "z_inverse": scatter_about(key_of[1], (NZ, NZ), NZ ** -0.5, 0.1875, (), jnp.float32),
        "tiles": draw_tiles(jax.random.fold_in(key_of[8], 71), 0),
        "amplitude": scatter_about(key_of[3], (BLOCKS, K, BLOCK), K ** -0.5, 3.0, ((0, 32),), jnp.float32),
        "lateral": scatter_about(key_of[4], (BLOCKS, TY, BLOCK), TY ** -0.5, 2.0, ((0, 32),), jnp.float32),
        "vertical": scatter_about(key_of[5], (BLOCKS, TZ, BLOCK), TZ ** -0.5, 0.375, ((0, 32),), jnp.float32),
        "wall_velocity": scatter_about(key_of[6], (BLOCKS, 3, BLOCK), 1.0, 6.0, ((0, 32),), jnp.float32),
        "surface": jnp.clip(jnp.exp(math.log(2.0) - 1.3862944 * jax.random.uniform(key_of[7], (BLOCKS, BLOCK), jnp.float32) ** levels(key_of[7], (BLOCKS, BLOCK), ((0, 32),), -0.2, 0.2)), 0.5, 2.0),
    }


smoothing = 1.0

def reference(velocity, z_inverse, tiles, amplitude, lateral, vertical, wall_velocity, surface):
    view = velocity.reshape(3, XW, NY // TY, TY, N_ROW, TZ).transpose(4, 1, 2, 0, 3, 5)
    block_rows = (jnp.arange(BLOCKS, dtype=jnp.int32) // (BLK_DEV * N_COL))[:, None]
    holder = tiles // T_DEV
    within = tiles % T_DEV
    plane = within // YTD
    band = holder * YTD + within % YTD
    picked = view[block_rows, plane, band]
    inner = jnp.einsum('bkcyz,bzi->bkcyi', picked, vertical, precision=lax.Precision.HIGHEST)
    weight = amplitude[:, :, None, :] * lateral[:, None, :, :]
    sampled = lax.optimization_barrier(jnp.sum(weight[:, :, None] * inner, axis=(1, 3)))
    marker_force = wall_velocity - sampled
    share = weight[:, :, None] * (surface[:, None, :] * marker_force)[:, None, :, None, :]
    spread = jnp.einsum('bkcyi,bzi->bkcyz', share, vertical, precision=lax.Precision.HIGHEST)
    forced_view = view.at[block_rows, plane, band].add(spread)
    forced = forced_view.transpose(3, 1, 2, 4, 0, 5).reshape(3, XW, NY, NZ)
    wave = jnp.arange(NY // 2).astype(jnp.float32)
    damping = 1.0 / (1.0 + 4.0 * smoothing * jnp.sin(jnp.pi * wave / NY) ** 2) / jnp.sqrt(jnp.float32(NY))

    def one_component(field):
        solved = jnp.einsum('xyz,zw->xyw', field, z_inverse, precision=lax.Precision.HIGHEST)
        modes = jnp.fft.rfft(solved, axis=1)[:, :NY // 2, :]
        scaled = modes * damping[None, :, None]
        return jnp.stack([jnp.real(scaled), jnp.imag(scaled)]).transpose(0, 1, 3, 2)
    spectra = lax.map(one_component, forced)
    spectrum = spectra.transpose(1, 0, 2, 3, 4)
    return (spectrum, marker_force)
```

```python
import jax
import jax.numpy as jnp
from jax import lax
from jax.experimental import pallas as pl
from jax.experimental.pallas import tpu as pltpu
from jax.sharding import PartitionSpec as P


TY = 8
K = 4
CAP = 8

smoothing = 1.0


f32 = jnp.float32
bf16 = jnp.bfloat16
ANY = pl.BlockSpec(memory_space=pl.ANY)
SMEM = pl.BlockSpec(memory_space=pltpu.SMEM)
VMEM = pl.BlockSpec(memory_space=pltpu.VMEM)
NT = (((1,), (1,)), ((), ()))
NN = (((1,), (0,)), ((), ()))


def split(x):
    hi = x.astype(bf16)
    return hi, (x - hi.astype(f32)).astype(bf16)


def dot3(a, b, dims):
    dot = lambda p, q: lax.dot_general(p, q, dims, preferred_element_type=f32)
    return dot(a[0], b[0]) + (dot(a[0], b[1]) + dot(a[1], b[0]))


def swap(x, axis, m, n):
    return lax.ppermute(x, axis, [(i, i ^ m) for i in range(n)])


def gather_tiles(meta, served, velocity, columns, per_row):
    comps, _, _, depth = velocity.shape

    def body(meta_ref, served_ref, vel, *rest):
        outs = rest[:columns]
        pool, sem_in, sem_out = rest[columns:]
        mine = meta_ref[1]
        order = list(range(columns))[::-1]
        loads = {}
        for m in order:
            for s in range(CAP):
                t = served_ref[mine ^ m, s]
                band = pl.multiple_of((t % per_row) * TY, TY)
                loads[m, s] = pltpu.make_async_copy(
                    vel.at[:, t // per_row, pl.ds(band, TY), :], pool.at[m, s], sem_in.at[m, s]
                )
                loads[m, s].start()
        stores = []
        for m in order:
            for s in range(CAP):
                loads[m, s].wait()
            stores.append(pltpu.make_async_copy(pool.at[m], outs[m], sem_out.at[m]))
            stores[-1].start()
        for cp in stores:
            cp.wait()

    return pl.pallas_call(
        body,
        in_specs=[SMEM, SMEM, ANY],
        out_specs=[ANY] * columns,
        out_shape=[jax.ShapeDtypeStruct((CAP, comps, TY, depth), f32)] * columns,
        scratch_shapes=[
            pltpu.VMEM((columns, CAP, comps, TY, depth), f32),
            pltpu.SemaphoreType.DMA((columns, CAP)),
            pltpu.SemaphoreType.DMA((columns,)),
        ],
        name="gather_tiles",
    )(meta, served, velocity)


def markers(slot, fetched, amplitude, lateral, vertical, wall, surface):
    columns = len(fetched)
    blocks, _, count = amplitude.shape
    _, comps, _, depth = fetched[0].shape
    rows = comps * TY

    def body(slot_ref, *refs):
        ins = refs[:columns]
        amp, lat, ver, wal, sur = refs[columns : columns + 5]
        outs = refs[columns + 5 : 2 * columns + 5]
        force = refs[2 * columns + 5]
        tin, tout, sem_in, sem_out = refs[2 * columns + 6 :]
        loads = [
            pltpu.make_async_copy(ins[m], tin.at[pl.ds(m * CAP, CAP)], sem_in.at[m])
            for m in range(columns)
        ]
        for cp in loads:
            cp.start()
        tout[...] = jnp.zeros(tout.shape, f32)
        for cp in loads:
            cp.wait()
        for b in range(blocks):
            v = split(ver[b])
            weight = [amp[b, k : k + 1, :] * lat[b] for k in range(K)]
            picked = jnp.concatenate(
                [tin[slot_ref[b * K + k]].reshape(rows, depth) for k in range(K)], axis=0
            )
            inner = dot3(split(picked), v, NN)
            shares = [[None] * comps for _ in range(K)]
            for c in range(comps):
                total = jnp.zeros((TY, count), f32)
                for k in range(K):
                    at = k * rows + c * TY
                    total = total + weight[k] * inner[at : at + TY]
                mf = wal[b, c : c + 1, :] - jnp.sum(total, axis=0, keepdims=True)
                force[b, c : c + 1, :] = mf
                scaled = sur[b : b + 1, :] * mf
                for k in range(K):
                    shares[k][c] = weight[k] * scaled
            share = jnp.concatenate([shares[k][c] for k in range(K) for c in range(comps)], axis=0)
            spread = dot3(split(share), v, NT)
            for k in range(K):
                tout[slot_ref[b * K + k]] = spread[k * rows : (k + 1) * rows].reshape(
                    comps, TY, depth
                )
        stores = [
            pltpu.make_async_copy(tout.at[pl.ds(m * CAP, CAP)], outs[m], sem_out.at[m])
            for m in range(columns)
        ]
        for cp in stores[::-1]:
            cp.start()
        for cp in stores:
            cp.wait()

    tile = (CAP, comps, TY, depth)
    pool = pltpu.VMEM((columns * CAP, comps, TY, depth), f32)
    out = pl.pallas_call(
        body,
        in_specs=[SMEM] + [ANY] * columns + [VMEM] * 5,
        out_specs=[ANY] * columns + [VMEM],
        out_shape=[jax.ShapeDtypeStruct(tile, f32)] * columns
        + [jax.ShapeDtypeStruct(wall.shape, f32)],
        scratch_shapes=[
            pool,
            pool,
            pltpu.SemaphoreType.DMA((columns,)),
            pltpu.SemaphoreType.DMA((columns,)),
        ],
        name="markers",
    )(slot, *fetched, amplitude, lateral, vertical, wall, surface)
    return out[:columns], out[columns]


def fill(meta, served, incoming, velocity, chunk, rows_n, per_row, after):
    columns = len(incoming)
    _, width_x, height, depth = velocity.shape
    xl, c0, nc = chunk
    planes = width_x // rows_n
    extra = len(after)

    def body(meta_ref, served_ref, *refs):
        ins = refs[:columns]
        vel = refs[columns]
        rest = refs[columns + 1 + extra :]
        outs = rest[:rows_n]
        buf, inc, sem_in, sem_v, sem_out = rest[rows_n:]
        me, mine = meta_ref[0], meta_ref[1]
        loads = []
        for m in range(rows_n):
            cp = pltpu.make_async_copy(
                vel.at[pl.ds(c0, nc), (me ^ m) * planes + xl], buf.at[m], sem_v.at[m]
            )
            cp.start()
            loads.append(cp)
        for m in range(columns):
            cp = pltpu.make_async_copy(
                ins[m].at[:, pl.ds(c0, nc)], inc.at[pl.ds(m * CAP, CAP)], sem_in.at[m]
            )
            cp.start()
            loads.append(cp)
        for cp in loads:
            cp.wait()

        def add(s, carry):
            t = served_ref[mine ^ (s // CAP), s % CAP]
            plane = t // per_row
            band = pl.multiple_of((t % per_row) * TY, TY)

            @pl.when(plane % planes == xl)
            def _():
                to = (plane // planes) ^ me
                buf[to, :, pl.ds(band, TY), :] += inc[s]

            return carry

        lax.fori_loop(0, columns * CAP, add, 0)
        stores = [pltpu.make_async_copy(buf.at[m], outs[m], sem_out.at[m]) for m in range(rows_n)]
        for cp in stores[::-1]:
            cp.start()
        for cp in stores:
            cp.wait()

    return pl.pallas_call(
        body,
        in_specs=[SMEM, SMEM] + [ANY] * (columns + 1 + extra),
        out_specs=[ANY] * rows_n,
        out_shape=[jax.ShapeDtypeStruct((nc, height, depth), f32)] * rows_n,
        scratch_shapes=[
            pltpu.VMEM((rows_n, nc, height, depth), f32),
            pltpu.VMEM((columns * CAP, nc, TY, depth), f32),
            pltpu.SemaphoreType.DMA((columns,)),
            pltpu.SemaphoreType.DMA((rows_n,)),
            pltpu.SemaphoreType.DMA((rows_n,)),
        ],
        name="fill",
    )(meta, served, *incoming, velocity, *after)


def axial_weights(meta, z_inverse, rows_n, columns, after):
    total = z_inverse.shape[0]
    depth, width = total // rows_n, total // columns
    extra = len(after)

    def body(meta_ref, z, *rest):
        hi, lo = rest[extra:]
        a, b = split(z[...].T)
        hi[...] = a
        lo[...] = b

    grid_spec = pltpu.PrefetchScalarGridSpec(
        num_scalar_prefetch=1,
        grid=(columns // 2, rows_n),
        in_specs=[
            pl.BlockSpec((depth, 2 * width), lambda o, i, s: (s[0] ^ i, (s[1] // 2) ^ o))
        ]
        + [ANY] * extra,
        out_specs=[pl.BlockSpec((2 * width, depth), lambda o, i, s: (o, i))] * 2,
    )
    return pl.pallas_call(
        body,
        grid_spec=grid_spec,
        out_shape=[jax.ShapeDtypeStruct((total, total), bf16)] * 2,
        name="axial_weights",
    )(meta, z_inverse, *after)


def solve(meta, planes, weights, after):
    rows_n = len(planes)
    extra = len(after)
    nc, height, depth = planes[0].shape
    total = weights[0].shape[0]
    columns = meta[1]
    width = total // columns

    def body(meta_ref, *refs):
        ins = refs[:rows_n]
        hi, lo = refs[rows_n : rows_n + 2]
        outs = refs[rows_n + 2 + extra : rows_n + 2 + extra + columns]
        fh, fl = refs[rows_n + 2 + extra + columns :]
        for m in range(rows_n):
            a, b = split(ins[m][0])
            fh[:, m * depth : (m + 1) * depth] = a
            fl[:, m * depth : (m + 1) * depth] = b
        field = (fh[...], fl[...])
        odd = meta_ref[1] % 2
        for o in range(columns // 2):
            got = dot3(
                (hi[o * 2 * width : (o + 1) * 2 * width], lo[o * 2 * width : (o + 1) * 2 * width]),
                field,
                NT,
            )
            first, second = got[:width], got[width:]
            outs[2 * o][0] = jnp.where(odd == 0, first, second)
            outs[2 * o + 1][0] = jnp.where(odd == 0, second, first)

    return pl.pallas_call(
        body,
        grid=(nc,),
        in_specs=[SMEM]
        + [pl.BlockSpec((1, height, depth), lambda u: (u, 0, 0))] * rows_n
        + [pl.BlockSpec((total, total), lambda u: (0, 0))] * 2
        + [ANY] * extra,
        out_specs=[pl.BlockSpec((1, width, height), lambda u: (u, 0, 0))] * columns,
        out_shape=[jax.ShapeDtypeStruct((nc, width, height), f32)] * columns,
        scratch_shapes=[pltpu.VMEM((height, total), bf16)] * 2,
        name="solve",
    )(meta[0], *planes, *weights, *after)


def fourier_table(ny, blocks, after):
    half = ny // 2
    height = half // blocks
    wavenumber = jnp.arange(half, dtype=jnp.int32)

    def waves(places):
        phase = (places[:, None] * wavenumber[None, :] % ny).astype(f32) * (2.0 * jnp.pi / ny)
        return jnp.cos(phase), jnp.sin(phase)

    wave = wavenumber.astype(f32)
    damping = 1.0 / (1.0 + 4.0 * smoothing * jnp.sin(jnp.pi * wave / ny) ** 2) / jnp.sqrt(f32(ny))
    coarse = waves(jnp.arange(blocks, dtype=jnp.int32) * height)
    fine = waves(jnp.arange(height, dtype=jnp.int32))
    fine = (fine[0] * damping[None, :], fine[1] * damping[None, :])
    middle = jnp.where(wavenumber % 2 == 0, damping, -damping)[None, :]
    block = min(half, 512)
    per = half // block
    extra = len(after)

    def body(cc, cs, fc, fs, *rest):
        hi, lo = rest[extra:]
        p = pl.program_id(1)
        a, b = cc[0], cs[0]

        @pl.when(p == 0)
        def _():
            hi[...], lo[...] = split(a * fc[...] - b * fs[...])

        @pl.when(p == 1)
        def _():
            hi[...], lo[...] = split(-(b * fc[...] + a * fs[...]))

    coarse_spec = pl.BlockSpec((1, 1, block), lambda n, p, m: (m, 0, n))
    fine_spec = pl.BlockSpec((height, block), lambda n, p, m: (0, n))
    hi, lo = pl.pallas_call(
        body,
        grid=(per, 2, blocks),
        in_specs=[coarse_spec, coarse_spec, fine_spec, fine_spec] + [ANY] * extra,
        out_specs=[pl.BlockSpec((height, block), lambda n, p, m: (m, p * per + n))] * 2,
        out_shape=[jax.ShapeDtypeStruct((half, ny), bf16)] * 2,
        name="fourier_table",
    )(coarse[0][:, None, :], coarse[1][:, None, :], *fine, *after)
    return hi, lo, middle


def transform(meta, pieces, table, chunk, shape, spectrum, after):
    columns = len(pieces)
    nc, width, height = pieces[0].shape
    ny = height * columns
    half = ny // 2
    low = columns // 2
    rows = nc * width
    xl, c0, _ = chunk
    block = min(half, 256)
    per = half // block
    carried = [] if spectrum is None else [spectrum]
    extra = len(after) + len(carried)

    def body(meta_ref, *refs):
        ins = refs[:columns]
        hi, lo, mid = refs[columns : columns + 3]
        out, held, eh, el, oh, ol, alone = refs[columns + 3 + extra :]
        mine = meta_ref[1]
        n = pl.program_id(0)

        @pl.when(n == 0)
        def _():
            for m in range(columns):
                held[mine ^ m] = ins[m][...].reshape(rows, height)
            lane = lax.broadcasted_iota(jnp.int32, (height, height), 1)
            sub = lax.broadcasted_iota(jnp.int32, (height, height), 0)
            turn = jnp.where(lane + sub == height, 1.0, 0.0).astype(bf16)
            first = lax.broadcasted_iota(jnp.int32, (rows, height), 1) == 0
            for q in range(low):
                a, b = split(held[columns - 1 - q])
                dot = lambda x: lax.dot_general(x, turn, NN, preferred_element_type=f32)
                back = dot(a) + dot(b)
                edge = held[columns - q] if q > 0 else jnp.zeros((rows, height), f32)
                back = jnp.where(first, edge, back)
                here = held[q]
                at = slice(q * height, (q + 1) * height)
                eh[:, at], el[:, at] = split(here + back)
                oh[:, at], ol[:, at] = split(here - back)
            alone[...] = jnp.broadcast_to(held[low][:, 0:1], alone.shape)

        @pl.when(n < per)
        def _():
            got = dot3((eh[...], el[...]), (hi[...], lo[...]), NN)
            got = got + alone[:, 0:1] * mid[...]
            out[...] = got.reshape(1, nc, 1, width, block)

        @pl.when(n >= per)
        def _():
            got = dot3((oh[...], ol[...]), (hi[...], lo[...]), NN)
            out[...] = got.reshape(1, nc, 1, width, block)

    return pl.pallas_call(
        body,
        grid=(2 * per,),
        in_specs=[SMEM]
        + [pl.BlockSpec((nc, width, height), lambda n: (0, 0, 0))] * columns
        + [pl.BlockSpec((half, block), lambda n: (0, n))] * 2
        + [pl.BlockSpec((1, block), lambda n: (0, n % per))]
        + [ANY] * extra,
        out_specs=pl.BlockSpec(
            (1, nc, 1, width, block), lambda n: (n // per, c0 // nc, xl, 0, n % per)
        ),
        out_shape=jax.ShapeDtypeStruct(shape, f32),
        scratch_shapes=[pltpu.VMEM((columns, rows, height), f32)]
        + [pltpu.VMEM((rows, half), bf16)] * 4
        + [pltpu.VMEM((rows, 128), f32)],
        input_output_aliases={columns + 4: 0} if carried else {},
        name="transform",
    )(meta, *pieces, *table, *carried, *after)


def chunks_of(comps, planes):
    last = planes - 1
    parts = [(0, comps - 1, 1), (0, 0, comps - 1)]
    parts += [(x, 0, comps) for x in range(1, last)]
    parts += [(last, 0, comps - 1), (last, comps - 1, 1)]
    return parts


def local(velocity, z_inverse, tiles, amplitude, lateral, vertical, wall_velocity, surface):
    comps, width_x, height, depth = velocity.shape
    columns = lax.axis_size("col")
    rows_n = lax.axis_size("row")
    me = lax.axis_index("row").astype(jnp.int32)
    mine = lax.axis_index("col").astype(jnp.int32)
    meta = jnp.stack([me, mine])
    per_row = height // TY
    tile_count = width_x * per_row
    requests = tiles.reshape(-1)
    count = requests.shape[0]
    holder = requests // tile_count
    within = requests % tile_count
    order = jnp.arange(count, dtype=jnp.int32)
    place = jnp.sum(
        ((holder[:, None] == holder[None, :]) & (order[None, :] < order[:, None])).astype(
            jnp.int32
        ),
        axis=1,
    )
    lanes = 128
    who = jnp.arange(columns, dtype=jnp.int32)[:, None, None]
    spot = jnp.arange(lanes, dtype=jnp.int32)[None, :, None]
    hit = (holder[None, None, :] == who) & (place[None, None, :] == spot)
    wanted = jnp.sum(jnp.where(hit, within[None, None, :], 0), axis=2)
    slot = (holder ^ mine) * CAP + place
    served = lax.all_to_all(wanted, "col", split_axis=0, concat_axis=0, tiled=True)
    asked = gather_tiles(meta, served, velocity, columns, per_row)
    fetched = [asked[0]] + [None] * (columns - 1)
    for m in reversed(range(1, columns)):
        fetched[m] = swap(asked[m], "col", m, columns)
    weights = axial_weights(meta, z_inverse, rows_n, columns, [asked[0]])
    outgoing, marker_force = markers(
        slot, fetched, amplitude, lateral, vertical, wall_velocity, surface
    )
    incoming = [outgoing[0]] + [None] * (columns - 1)
    for m in reversed(range(1, columns)):
        incoming[m] = swap(outgoing[m], "col", m, columns)
    table = fourier_table(height * columns, max(columns // 2, 1), [outgoing[0]])
    planes = width_x // rows_n
    chunks = chunks_of(comps, planes)
    solved = []
    sent = [None] * len(chunks)
    got = [None] * len(chunks)

    def send(j, after):
        sent[j] = fill(meta, served, incoming, velocity, chunks[j], rows_n, per_row, after)
        got[j] = [sent[j][0]] + [None] * (rows_n - 1)
        for m in reversed(range(1, rows_n)):
            got[j][m] = swap(sent[j][m], "row", m, rows_n)

    send(0, [weights[0], table[0]])
    send(1, [sent[0][0]])
    for j in range(len(chunks)):
        ahead = [sent[j + 1][0]] if j + 1 < len(chunks) else []
        out = solve((meta, columns), got[j], weights, ahead)
        pieces = [out[0]] + [None] * (columns - 1)
        for m in reversed(range(1, columns)):
            pieces[m] = swap(out[m], "col", m, columns)
        solved.append(pieces)
        if j + 2 < len(chunks):
            send(j + 2, [out[0]])
    last = [solved[-1][0]]
    total = depth * rows_n
    shape = (2, comps, planes, total // columns, height * columns // 2)
    spectrum = None
    for j in range(len(chunks)):
        spectrum = transform(
            meta, solved[j], table, chunks[j], shape, spectrum, last if j == 0 else []
        )
    return (spectrum, marker_force)


def solution(mesh):
    in_specs = (
        P(None, None, "col", "row"),
        P(),
        P(("row", "col"), None),
        P(("row", "col"), None, None),
        P(("row", "col"), None, None),
        P(("row", "col"), None, None),
        P(("row", "col"), None, None),
        P(("row", "col"), None),
    )
    out_specs = (P(None, None, "row", "col", None), P(("row", "col"), None, None))

    return jax.shard_map(local, mesh=mesh, in_specs=in_specs, out_specs=out_specs, check_vma=False)
```
